32 devices in a mesh: ctx: 16 (over z, x, core), head: 2 (over y).
Axes of the slice: x: 2, y: 2, z: 4, core: 2. Of those that a mesh axis runs over, the one named last changes fastest.
Arguments:
- latent: bfloat16 [6144, 5120], P('ctx', 'head'), may hold values from -6 to 6
- probe: bfloat16 [6144, 5120], P('ctx'), may hold values from -6 to 6
- norm_gain: float32 [5120], replicated, may hold values from 0.25 to 1.75
- w_query: bfloat16 [5120, 3072], P('ctx', 'head'), may hold values from -2 to 2, as said below
- w_key: bfloat16 [5120, 3072], P('ctx', 'head'), may hold values from -2 to 2, as said below
- w_value: bfloat16 [5120, 3072], P('ctx', 'head'), may hold values from -0.078125 to 0.078125
- w_out: bfloat16 [3072, 5120], P('head', 'ctx'), may hold values from -0.109375 to 0.109375
- tile_mask: int32 [48, 48], replicated, may hold values from 0 to 1, as said below
Outputs:
- mixed: bfloat16 [6144, 5120], P('ctx', 'head')
- branch_tangent: bfloat16 [6144, 5120], P('ctx', 'head')
- trace_terms: float32 [6144], P('ctx')
The draws below stay inside these ranges and needn't reach their ends.
Inputs may be any that keep to these rules, and one draw needn't show every extreme that they name: `tile_mask`: entry [q, k] is 0 where |q - k| > 3, and 1 where q == k or |q - k| == 3. `w_query`: entries of order 5120^-0.5. `w_key`: entries of order 5120^-0.5.
All inputs are finite; a program needn't handle non-finite values.
Results may differ from the reference program's by a relative error of at most 0.011.
Values may be sent and summed in bfloat16 or wider, within the bound.
A program may use at most 192 MiB of HBM per device.

```python
import jax
import jax.numpy as jnp
from jax import lax

D = 5120
HD = 128
HEADS = 24
TILE = 128
TILES_DEV = 3
TOK_DEV = 384
TOKENS = 6144
NT = 48
N_CTX = 16
N_HEAD = 2


def pair_weights(key):
    base = jax.random.fold_in(key, 11)
    shared = jnp.clip(jax.random.normal(jax.random.fold_in(base, 1), (D, HEADS * HD), jnp.float32), -6.0, 6.0)
    others = jnp.clip(jax.random.normal(jax.random.fold_in(base, 2), (D, HEADS * HD), jnp.float32), -6.0, 6.0)
    return (shared, others)


def draw_w_key(key, part):
    shared, others = pair_weights(key)
    return jnp.clip(shared * D ** (-0.5), -2.0, 2.0).astype(jnp.bfloat16)


def draw_w_query(key, part):
    shared, others = pair_weights(key)
    blended = others
    return jnp.clip(blended * D ** (-0.5), -2.0, 2.0).astype(jnp.bfloat16)


def draw_tile_mask(key, part):
    rows_idx = jnp.arange(NT, dtype=jnp.int32)[:, None]
    cols_idx = jnp.arange(NT, dtype=jnp.int32)[None, :]
    levels = jax.random.randint(jax.random.fold_in(key, 1), (NT // TILES_DEV,), 1, 5)
    row_level = levels[rows_idx // TILES_DEV]
    coins = jax.random.randint(jax.random.fold_in(key, 2), (NT, NT), 0, 4)
    keeper = coins < row_level
    distance = jnp.abs(rows_idx - cols_idx)
    banded = distance <= TILES_DEV
    forced = (distance == 0) | (distance == TILES_DEV)
    return jnp.where(banded & (keeper | forced), 1, 0).astype(jnp.int32)


def shard_levels(own_key, dims, pieces, smallest, largest):
    gain = 1.0
    for dim, parts in pieces:
        steps = jax.random.uniform(jax.random.fold_in(jax.random.fold_in(own_key, 6), dim), (parts,), jnp.float32, smallest / len(pieces), largest / len(pieces))
        gain = gain * jnp.repeat(jnp.exp(steps), dims[dim] // parts).reshape((-1,) + (1,) * (len(dims) - 1 - dim))
    return gain


def centred(stream_key, dims, deviation, most, cuts=(), kind=jnp.bfloat16):
    drawn = deviation * jax.random.normal(stream_key, dims, jnp.float32)
    if cuts:
        drawn = drawn * shard_levels(stream_key, dims, cuts, -0.22, 0.18)
    return jnp.clip(drawn, -most, most).astype(kind)


def setup_inputs(seed: int = 0) -> dict:
    arg_keys = jax.random.split(jax.random.key(seed), 9)
    return {
        "latent": centred(arg_keys[0], (TOKENS, D), 1.0, 6.0, ((0, 16), (1, 2))),
        "probe": centred(arg_keys[1], (TOKENS, D), 1.0, 6.0, ((0, 16),)),
        "norm_gain": jnp.clip(1.0 + 0.15 * jax.random.normal(arg_keys[2], (D,), jnp.float32), 0.25, 1.75),
        "w_query": draw_w_query(jax.random.fold_in(arg_keys[8], 71), 0),
        "w_key": draw_w_key(jax.random.fold_in(arg_keys[8], 71), 0),
        "w_value": centred(arg_keys[5], (D, HEADS * HD), D ** -0.5, 0.078125, ((0, 16), (1, 2))),
        "w_out": centred(arg_keys[6], (HEADS * HD, D), (HEADS * HD) ** -0.5, 0.109375, ((0, 2), (1, 16))),
        "tile_mask": draw_tile_mask(jax.random.fold_in(arg_keys[8], 71), 0),
    }


def attend_block(queries, queries_t, keys, values, keys_t, values_t, allowed):
    score_scale = HD ** (-0.5)
    scores = jnp.einsum('qhd,khd->hqk', queries.astype(jnp.float32), keys.astype(jnp.float32)) * score_scale
    masked = jnp.where(allowed[None], scores, -jnp.inf)
    highest = lax.optimization_barrier(jnp.max(masked, -1, keepdims=True))
    expos = jnp.exp(masked - highest)
    probs = expos / lax.optimization_barrier(jnp.sum(expos, -1, keepdims=True))
    scores_t = jnp.einsum('qhd,khd->hqk', queries_t.astype(jnp.float32), keys.astype(jnp.float32))
    scores_t = (scores_t + jnp.einsum('qhd,khd->hqk', queries.astype(jnp.float32), keys_t.astype(jnp.float32))) * score_scale
    probs_t = probs * (scores_t - lax.optimization_barrier(jnp.sum(probs * scores_t, -1, keepdims=True)))
    probs_b = probs.astype(jnp.bfloat16).astype(jnp.float32)
    probs_tb = probs_t.astype(jnp.bfloat16).astype(jnp.float32)
    attended = jnp.einsum('hqk,khd->qhd', probs_b, values.astype(jnp.float32)).astype(jnp.bfloat16)
    attended_t = jnp.einsum('hqk,khd->qhd', probs_b, values_t.astype(jnp.float32))
    attended_t = (attended_t + jnp.einsum('hqk,khd->qhd', probs_tb, values.astype(jnp.float32))).astype(jnp.bfloat16)
    return (attended, attended_t)

def reference(latent, probe, norm_gain, w_query, w_key, w_value, w_out, tile_mask):
    tangent = probe.astype(jnp.float32)
    latent_f = latent.astype(jnp.float32)
    inverse = lax.rsqrt(lax.optimization_barrier(jnp.sum(latent_f * latent_f, -1, keepdims=True)) / D + 1e-06)
    along = lax.optimization_barrier(jnp.sum(latent_f * tangent, -1, keepdims=True)) / D
    normed = (latent_f * inverse * norm_gain).astype(jnp.bfloat16)
    normed_t = ((tangent * inverse - latent_f * inverse ** 3 * along) * norm_gain).astype(jnp.bfloat16)

    def project(weight):
        first = jnp.dot(normed, weight, preferred_element_type=jnp.float32).astype(jnp.bfloat16)
        second = jnp.dot(normed_t, weight, preferred_element_type=jnp.float32).astype(jnp.bfloat16)
        return (first.reshape(TOKENS, HEADS, HD), second.reshape(TOKENS, HEADS, HD))
    query, query_t = project(w_query)
    key_all, key_t = project(w_key)
    value_all, value_t = project(w_value)

    def padded(field):
        return jnp.pad(field, ((TOK_DEV, TOK_DEV), (0, 0), (0, 0)))
    key_pad, key_t_pad = (padded(key_all), padded(key_t))
    value_pad, value_t_pad = (padded(value_all), padded(value_t))
    mask_pad = jnp.pad(tile_mask, TILES_DEV)

    def shard_attend(shard):
        first = shard * TOK_DEV
        queries = lax.dynamic_slice_in_dim(query, first, TOK_DEV, 0)
        queries_t = lax.dynamic_slice_in_dim(query_t, first, TOK_DEV, 0)
        keys = lax.dynamic_slice_in_dim(key_pad, first, 3 * TOK_DEV, 0)
        keys_t = lax.dynamic_slice_in_dim(key_t_pad, first, 3 * TOK_DEV, 0)
        values = lax.dynamic_slice_in_dim(value_pad, first, 3 * TOK_DEV, 0)
        values_t = lax.dynamic_slice_in_dim(value_t_pad, first, 3 * TOK_DEV, 0)
        tile_rows = lax.dynamic_slice(mask_pad, (shard * TILES_DEV + TILES_DEV, shard * TILES_DEV), (TILES_DEV, 3 * TILES_DEV))
        allowed = jnp.repeat(jnp.repeat(tile_rows, TILE, 0), TILE, 1) == 1
        return attend_block(queries, queries_t, keys, values, keys_t, values_t, allowed)
    attended, attended_t = lax.map(shard_attend, jnp.arange(N_CTX, dtype=jnp.int32))
    attended = attended.reshape(TOKENS, HEADS * HD)
    attended_t = attended_t.reshape(TOKENS, HEADS * HD)
    group = HEADS * HD // N_HEAD
    branch = jnp.zeros((TOKENS, D), jnp.float32)
    branch_t = jnp.zeros((TOKENS, D), jnp.float32)
    for member in range(N_HEAD):
        rows_out = w_out[member * group:(member + 1) * group]
        part_one = jnp.dot(attended[:, member * group:(member + 1) * group], rows_out, preferred_element_type=jnp.float32)
        part_two = jnp.dot(attended_t[:, member * group:(member + 1) * group], rows_out, preferred_element_type=jnp.float32)
        part_one = lax.optimization_barrier(part_one.astype(jnp.bfloat16))
        part_two = lax.optimization_barrier(part_two.astype(jnp.bfloat16))
        branch = branch + part_one.astype(jnp.float32)
        branch_t = branch_t + part_two.astype(jnp.float32)
    mixed = (latent_f + branch).astype(jnp.bfloat16)
    trace_terms = lax.optimization_barrier(jnp.sum(tangent * branch_t, -1))
    return (mixed, branch_t.astype(jnp.bfloat16), trace_terms)
```

```python
import functools

import jax
import jax.numpy as jnp
from jax import lax
from jax.experimental import pallas as pl
from jax.experimental.pallas import tpu as pltpu
from jax.sharding import PartitionSpec as P

D = 5120
HD = 128
TILE = 128
MESH = pl.DeviceIdType.MESH
MIB = 1 << 20


def chip_of(pos, chips):
    half = pos // (chips // 2)
    return (1 - half) * 2 * pos + half * (2 * (chips - 1 - pos) + 1)


def project_kernel(
    n, heads, lat_ref, probe_ref, gain_ref, w_ref,
    qkv_ref, wo_ref, proj_ref, halo_ref,
    lat_all, x_ref, wbuf, obuf,
    local_sem, ring_send, ring_recv, flip_send, flip_recv, own_send, own_recv,
    lat_send, lat_recv, lat_local, load_sem, store_sem, halo_send, halo_recv, halo_local,
):
    chips = n // 2
    hops = chips - 1
    tok, own = lat_ref.shape
    cols = proj_ref.shape[-1]
    width = wbuf.shape[-1]
    pieces = cols // width
    me = lax.axis_index("ctx")
    head = lax.axis_index("head")
    core = me % 2
    chip = me // 2
    cx = chip % 2
    cz = chip // 2
    pos = (1 - cx) * cz + cx * (chips - 1 - cz)
    ahead = chip_of((pos + 1) % chips, chips) * 2 + core
    behind = chip_of((pos + chips - 1) % chips, chips) * 2 + core
    twin = me + 1 - 2 * core
    right = (me + 1) % n
    left = (me + n - 1) % n

    barrier = pltpu.get_barrier_semaphore()
    for other in (ahead, behind, twin, right, left):
        pl.semaphore_signal(barrier, inc=1, device_id={"ctx": other}, device_id_type=MESH)
    for k in range(1, heads):
        pl.semaphore_signal(
            barrier, inc=1, device_id={"head": (head + k) % heads}, device_id_type=MESH
        )

    def full(w):
        return wo_ref if w == 3 else qkv_ref.at[w]

    def local_copy(w):
        return pltpu.make_async_copy(w_ref.at[w], full(w).at[me], local_sem.at[w])

    for w in range(4):
        local_copy(w).start()
    mine = pltpu.make_async_copy(lat_ref, lat_all.at[head], lat_local)
    mine.start()
    pl.semaphore_wait(barrier, 5 + heads - 1)

    def ring(w, hop, way):
        source = (pos + chips - hop) % chips if way == 0 else (pos + hop) % chips
        owner = chip_of(source, chips) * 2 + core
        block = full(w).at[owner, way]
        return pltpu.make_async_remote_copy(
            src_ref=block, dst_ref=block,
            send_sem=ring_send.at[w, hop, way], recv_sem=ring_recv.at[w, hop, way],
            device_id={"ctx": ahead if way == 0 else behind}, device_id_type=MESH,
        )

    def arrived(w, hop, way):
        source = (pos + chips - hop - 1) % chips if way == 0 else (pos + hop + 1) % chips
        return full(w).at[chip_of(source, chips) * 2 + core, way]

    def ring_wait(w, hop, way):
        block = arrived(w, hop, way)
        pltpu.make_async_remote_copy(
            src_ref=block, dst_ref=block,
            send_sem=ring_send.at[w, hop, way], recv_sem=ring_recv.at[w, hop, way],
            device_id={"ctx": ahead if way == 0 else behind}, device_id_type=MESH,
        ).wait_recv()

    def flip(w, hop, way):
        block = arrived(w, hop, way)
        return pltpu.make_async_remote_copy(
            src_ref=block, dst_ref=block,
            send_sem=flip_send.at[w, hop, way], recv_sem=flip_recv.at[w, hop, way],
            device_id={"ctx": twin}, device_id_type=MESH,
        )

    def flip_wait(w, hop, way):
        source = (pos + chips - hop - 1) % chips if way == 0 else (pos + hop + 1) % chips
        block = full(w).at[chip_of(source, chips) * 2 + 1 - core, way]
        pltpu.make_async_remote_copy(
            src_ref=block, dst_ref=block,
            send_sem=flip_send.at[w, hop, way], recv_sem=flip_recv.at[w, hop, way],
            device_id={"ctx": twin}, device_id_type=MESH,
        ).wait_recv()

    def own_flip(w, who):
        block = full(w).at[who]
        return pltpu.make_async_remote_copy(
            src_ref=block, dst_ref=block,
            send_sem=own_send.at[w], recv_sem=own_recv.at[w],
            device_id={"ctx": twin}, device_id_type=MESH,
        )

    def begin(w):
        ring(w, 0, 0).start()
        ring(w, 0, 1).start()
        own_flip(w, me).start()

    def advance(w, hop):
        for way in range(2):
            ring_wait(w, hop - 1, way)
            ring(w, hop, way).start()
            flip(w, hop - 1, way).start()

    def finish(w):
        for way in range(2):
            ring_wait(w, hops - 1, way)
            flip(w, hops - 1, way).start()

    def settle(w):
        own_flip(w, twin).wait_recv()

        @pl.loop(0, hops)
        def _(hop):
            for way in range(2):
                flip_wait(w, hop, way)

    def drain(w):
        own_flip(w, me).wait_send()

        @pl.loop(0, hops)
        def _(hop):
            for way in range(2):
                ring(w, hop, way).wait_send()
                flip(w, hop, way).wait_send()

    def lat_copy(k):
        return pltpu.make_async_remote_copy(
            src_ref=lat_ref, dst_ref=lat_all.at[head],
            send_sem=lat_send.at[k - 1], recv_sem=lat_recv.at[k - 1],
            device_id={"head": (head + k) % heads}, device_id_type=MESH,
        )

    def norm():
        mine.wait()
        for k in range(1, heads):
            came = lat_all.at[(head + heads - k) % heads]
            pltpu.make_async_remote_copy(
                src_ref=lat_ref, dst_ref=came,
                send_sem=lat_send.at[k - 1], recv_sem=lat_recv.at[k - 1],
                device_id={"head": (head + k) % heads}, device_id_type=MESH,
            ).wait_recv()
        step = 16

        @pl.loop(0, tok // step)
        def _(i):
            rows = pl.ds(pl.multiple_of(i * step, step), step)
            squares = jnp.zeros((step, 1), jnp.float32)
            crossed = jnp.zeros((step, 1), jnp.float32)
            for h in range(heads):
                part = lat_all[h, rows, :].astype(jnp.float32)
                tang = probe_ref[rows, h * own:(h + 1) * own].astype(jnp.float32)
                squares = squares + jnp.sum(part * part, -1, keepdims=True)
                crossed = crossed + jnp.sum(part * tang, -1, keepdims=True)
            inverse = lax.rsqrt(squares / D + 1e-06)
            along = crossed / D
            second = inverse * inverse * inverse * along
            rows_t = pl.ds(pl.multiple_of(tok + i * step, step), step)
            for h in range(heads):
                part = lat_all[h, rows, :].astype(jnp.float32)
                tang = probe_ref[rows, h * own:(h + 1) * own].astype(jnp.float32)
                gain = gain_ref[:, h * own:(h + 1) * own]
                x_ref[rows, h * own:(h + 1) * own] = (part * inverse * gain).astype(jnp.bfloat16)
                x_ref[rows_t, h * own:(h + 1) * own] = (
                    (tang * inverse - part * second) * gain
                ).astype(jnp.bfloat16)

    def load(w, piece, slot):
        at = pl.ds(pl.multiple_of(piece * width, width), width)
        return pltpu.make_async_copy(
            qkv_ref.at[w, :, :, :, at], wbuf.at[slot], load_sem.at[slot]
        )

    def multiply(w, piece, slot):
        load(w, piece, slot).wait()
        weight = wbuf[slot].reshape(D, width)
        rows = 128

        @pl.loop(0, 2 * tok // rows)
        def _(i):
            at = pl.ds(pl.multiple_of(i * rows, rows), rows)
            obuf[slot, at, :] = jnp.dot(
                x_ref[at, :], weight, preferred_element_type=jnp.float32
            ).astype(jnp.bfloat16)

        at = pl.ds(pl.multiple_of(piece * width, width), width)
        store = pltpu.make_async_copy(
            obuf.at[slot], proj_ref.at[w, :, at], store_sem.at[slot]
        )
        store.start()
        store.wait()

    def both(piece):
        load(0, piece, 0).start()
        load(1, piece, 1).start()
        multiply(0, piece, 0)
        multiply(1, piece, 1)

    def halo(side):
        return pltpu.make_async_remote_copy(
            src_ref=proj_ref.at[pl.ds(0, 2)], dst_ref=halo_ref.at[side],
            send_sem=halo_send.at[side], recv_sem=halo_recv.at[side],
            device_id={"ctx": right if side == 0 else left}, device_id_type=MESH,
        )

    def halo_fill(side):
        return pltpu.make_async_copy(
            proj_ref.at[pl.ds(0, 2)], halo_ref.at[side], halo_local
        )

    def halo_start():
        @pl.when(me < n - 1)
        def _():
            halo(0).start()

        @pl.when(me > 0)
        def _():
            halo(1).start()

        @pl.when(me == 0)
        def _():
            halo_fill(0).start()

        @pl.when(me == n - 1)
        def _():
            halo_fill(1).start()

    def halo_end():
        @pl.when(me < n - 1)
        def _():
            halo(0).wait_send()
            halo(1).wait_recv()

        @pl.when(me > 0)
        def _():
            halo(1).wait_send()
            halo(0).wait_recv()

        @pl.when(me == 0)
        def _():
            halo_fill(0).wait()

        @pl.when(me == n - 1)
        def _():
            halo_fill(1).wait()

    for w in range(4):
        local_copy(w).wait()
    begin(0)
    begin(1)
    for k in range(1, heads):
        lat_copy(k).start()

    @pl.loop(1, hops)
    def _(hop):
        advance(0, hop)
        advance(1, hop)

        @pl.when(hop == hops - 1)
        def _():
            norm()

    begin(2)
    begin(3)
    finish(0)
    finish(1)
    settle(0)
    settle(1)

    per = 3
    turns = -(-pieces // per)

    @pl.loop(1, hops)
    def _(hop):
        advance(2, hop)
        advance(3, hop)

        @pl.when(hop <= turns)
        def _():
            for j in range(per):
                piece = (hop - 1) * per + j
                if pieces % per:
                    pl.when(piece < pieces)(lambda piece=piece: both(piece))
                else:
                    both(piece)

        @pl.when(hop == turns + 1)
        def _():
            halo_start()

    finish(2)
    finish(3)
    settle(2)

    @pl.loop(0, pieces)
    def _(piece):
        load(2, piece, 0).start()
        multiply(2, piece, 0)

    settle(3)
    halo_end()
    for w in range(4):
        drain(w)
    for k in range(1, heads):
        lat_copy(k).wait_send()


def gather_and_project(latent, probe, gain, weights):
    n = lax.axis_size("ctx")
    heads = lax.axis_size("head")
    hops = n // 2 - 1
    tok, own = latent.shape
    rows, cols = weights.shape[1:]
    weights = weights.reshape(4, 2, rows // 2, cols)
    width = 256 if cols % 256 == 0 else 128
    dma = pltpu.SemaphoreType.DMA
    bf = jnp.bfloat16
    vmem = pl.BlockSpec(memory_space=pltpu.VMEM)
    anywhere = pl.BlockSpec(memory_space=pl.ANY)
    return pl.pallas_call(
        functools.partial(project_kernel, n, heads),
        out_shape=(
            jax.ShapeDtypeStruct((3, n, 2, rows // 2, cols), bf),
            jax.ShapeDtypeStruct((n, 2, rows // 2, cols), bf),
            jax.ShapeDtypeStruct((3, 2 * tok, cols), bf),
            jax.ShapeDtypeStruct((2, 2, 2 * tok, cols), bf),
        ),
        in_specs=[vmem, vmem, vmem, anywhere],
        out_specs=(anywhere,) * 4,
        scratch_shapes=[
            pltpu.VMEM((heads, tok, own), bf),
            pltpu.VMEM((2 * tok, D), bf),
            pltpu.VMEM((2, n, 2, rows // 2, width), bf),
            pltpu.VMEM((2, 2 * tok, width), bf),
            dma((4,)), dma((4, hops, 2)), dma((4, hops, 2)), dma((4, hops, 2)), dma((4, hops, 2)),
            dma((4,)), dma((4,)),
            dma((heads - 1,)), dma((heads - 1,)), dma, dma((2,)), dma((2,)),
            dma((2,)), dma((2,)), dma,
        ],
        compiler_params=pltpu.CompilerParams(
            collective_id=0, has_side_effects=True, vmem_limit_bytes=48 * MIB
        ),
    )(latent, probe, gain, weights)


def attend_kernel(tiles, mask_ref, q_ref, own_ref, low_ref, high_ref, out_ref, k_all, v_all):
    tok = tiles * TILE
    scale = HD ** (-0.5)
    for place, ref in enumerate((low_ref, own_ref, high_ref)):
        at = slice(place * tok, (place + 1) * tok)
        k_all[at, :HD] = ref[0, :tok, :]
        k_all[at, HD:] = ref[0, tok:, :]
        v_all[at, :HD] = ref[1, :tok, :]
        v_all[at, HD:] = ref[1, tok:, :]
    contract = (((1,), (1,)), ((), ()))
    band = 2 * tiles + 1
    for i in range(tiles):
        rows = slice(i * TILE, (i + 1) * TILE)
        rows_t = slice(tok + i * TILE, tok + (i + 1) * TILE)
        query = q_ref[0, rows, :]
        query_t = q_ref[0, rows_t, :]
        keys = k_all[i * TILE:(i + band) * TILE, :]
        scores = lax.dot_general(
            query, keys[:, :HD], contract, preferred_element_type=jnp.float32
        ) * scale
        scores_t = lax.dot_general(
            jnp.concatenate([query_t, query], 1), keys, contract,
            preferred_element_type=jnp.float32,
        ) * scale
        masked = jnp.concatenate(
            [
                jnp.where(
                    mask_ref[i, i + j] == 1, scores[:, j * TILE:(j + 1) * TILE], -1e30
                )
                for j in range(band)
            ],
            1,
        )
        highest = jnp.max(masked, -1, keepdims=True)
        expos = jnp.exp(masked - highest)
        probs = expos * (1.0 / jnp.sum(expos, -1, keepdims=True))
        weighed = probs * scores_t
        probs_t = weighed - probs * jnp.sum(weighed, -1, keepdims=True)
        probs_b = probs.astype(jnp.bfloat16)
        values = v_all[i * TILE:(i + band) * TILE, :]
        first = jnp.dot(probs_b, values, preferred_element_type=jnp.float32)
        second = first[:, HD:] + jnp.dot(
            probs_t.astype(jnp.bfloat16), values[:, :HD], preferred_element_type=jnp.float32
        )
        out_ref[rows, :] = first[:, :HD].astype(jnp.bfloat16)
        out_ref[rows_t, :] = second.astype(jnp.bfloat16)


def attend(tile_rows, proj, halo):
    rows, cols = proj.shape[1:]
    tok = rows // 2
    tiles = tok // TILE
    return pl.pallas_call(
        functools.partial(attend_kernel, tiles),
        grid=(cols // HD,),
        out_shape=jax.ShapeDtypeStruct((rows, cols), jnp.bfloat16),
        in_specs=[
            pl.BlockSpec(memory_space=pltpu.SMEM),
            pl.BlockSpec((1, rows, HD), lambda h: (2, 0, h)),
            pl.BlockSpec((2, rows, HD), lambda h: (0, 0, h)),
            pl.BlockSpec((None, 2, rows, HD), lambda h: (0, 0, 0, h)),
            pl.BlockSpec((None, 2, rows, HD), lambda h: (1, 0, 0, h)),
        ],
        out_specs=pl.BlockSpec((rows, HD), lambda h: (0, h)),
        scratch_shapes=[pltpu.VMEM((3 * tok, 2 * HD), jnp.bfloat16)] * 2,
        compiler_params=pltpu.CompilerParams(vmem_limit_bytes=32 * MIB),
    )(tile_rows, proj, proj, halo, halo)


def shards(latent, probe, norm_gain, w_query, w_key, w_value, w_out, tile_mask):
    tok_rows, own_cols = latent.shape
    weights = jnp.stack([w_key, w_value, w_query, w_out.T])
    _, wo_full, proj, halo = gather_and_project(latent, probe, norm_gain.reshape(1, D), weights)
    tiles_dev = tok_rows // TILE
    ctx_slot = lax.axis_index("ctx")
    mask_pad = jnp.pad(tile_mask, tiles_dev)
    tile_rows = lax.dynamic_slice(
        mask_pad,
        (ctx_slot * tiles_dev + tiles_dev, ctx_slot * tiles_dev),
        (tiles_dev, 3 * tiles_dev),
    )
    both_rows = attend(tile_rows, proj, halo)
    w_out_t = wo_full.reshape(D, w_out.shape[0])
    terms = lax.dot_general(
        both_rows, w_out_t, (((1,), (1,)), ((), ())), preferred_element_type=jnp.float32
    ).astype(jnp.bfloat16)
    summed = lax.psum_scatter(terms, "head", scatter_dimension=1, tiled=True).astype(jnp.float32)
    branch = summed[:tok_rows]
    branch_t = summed[tok_rows:]
    latent_f = latent.astype(jnp.float32)
    col_start = lax.axis_index("head") * own_cols
    tangent_own = lax.dynamic_slice_in_dim(probe, col_start, own_cols, 1).astype(jnp.float32)
    mixed = (latent_f + branch).astype(jnp.bfloat16)
    trace_terms = lax.psum(jnp.sum(tangent_own * branch_t, -1), "head")
    return (mixed, branch_t.astype(jnp.bfloat16), trace_terms)


def solution(mesh):
    placed = (
        P("ctx", "head"),
        P("ctx", None),
        P(),
        P("ctx", "head"),
        P("ctx", "head"),
        P("ctx", "head"),
        P("head", "ctx"),
        P(),
    )
    return jax.shard_map(
        shards,
        mesh=mesh,
        in_specs=placed,
        out_specs=(P("ctx", "head"), P("ctx", "head"), P("ctx")),
        check_vma=False,
    )
```

```python
import functools

import jax
import jax.numpy as jnp
from jax import lax
from jax.experimental import pallas as pl
from jax.experimental.pallas import tpu as pltpu
from jax.sharding import PartitionSpec as P

D = 5120
HD = 128
TILE = 128
MESH = pl.DeviceIdType.MESH
MIB = 1 << 20


def chip_of(pos, chips):
    half = pos // (chips // 2)
    return (1 - half) * 2 * pos + half * (2 * (chips - 1 - pos) + 1)


def project_kernel(
    n, heads, lat_ref, probe_ref, gain_ref, w_ref,
    qkv_ref, wo_ref, proj_ref, halo_ref,
    lat_all, x_ref, wbuf, obuf,
    local_sem, ring_send, ring_recv, flip_send, flip_recv, own_send, own_recv,
    lat_send, lat_recv, lat_local, load_sem, store_sem, halo_send, halo_recv, halo_local,
):
    chips = n // 2
    hops = chips - 1
    tok, own = lat_ref.shape
    cols = proj_ref.shape[-1]
    width = wbuf.shape[-1]
    pieces = cols // width
    me = lax.axis_index("ctx")
    head = lax.axis_index("head")
    core = me % 2
    chip = me // 2
    cx = chip % 2
    cz = chip // 2
    pos = (1 - cx) * cz + cx * (chips - 1 - cz)
    ahead = chip_of((pos + 1) % chips, chips) * 2 + core
    behind = chip_of((pos + chips - 1) % chips, chips) * 2 + core
    twin = me + 1 - 2 * core
    right = (me + 1) % n
    left = (me + n - 1) % n

    barrier = pltpu.get_barrier_semaphore()
    for other in (ahead, behind, twin, right, left):
        pl.semaphore_signal(barrier, inc=1, device_id={"ctx": other}, device_id_type=MESH)
    for k in range(1, heads):
        pl.semaphore_signal(
            barrier, inc=1, device_id={"head": (head + k) % heads}, device_id_type=MESH
        )

    def full(w):
        return wo_ref if w == 3 else qkv_ref.at[w]

    def local_copy(w):
        return pltpu.make_async_copy(w_ref.at[w], full(w).at[me], local_sem.at[w])

    for w in range(4):
        local_copy(w).start()
    mine = pltpu.make_async_copy(lat_ref, lat_all.at[head], lat_local)
    mine.start()
    pl.semaphore_wait(barrier, 5 + heads - 1)

    def ring(w, hop, way, first=False):
        source = (pos + chips - hop) % chips if way == 0 else (pos + hop) % chips
        owner = chip_of(source, chips) * 2 + core
        block = full(w).at[owner, way]
        return pltpu.make_async_remote_copy(
            src_ref=w_ref.at[w, way] if first else block, dst_ref=block,
            send_sem=ring_send.at[w, hop, way], recv_sem=ring_recv.at[w, hop, way],
            device_id={"ctx": ahead if way == 0 else behind}, device_id_type=MESH,
        )

    def arrived(w, hop, way):
        source = (pos + chips - hop - 1) % chips if way == 0 else (pos + hop + 1) % chips
        return full(w).at[chip_of(source, chips) * 2 + core, way]

    def ring_wait(w, hop, way):
        block = arrived(w, hop, way)
        pltpu.make_async_remote_copy(
            src_ref=block, dst_ref=block,
            send_sem=ring_send.at[w, hop, way], recv_sem=ring_recv.at[w, hop, way],
            device_id={"ctx": ahead if way == 0 else behind}, device_id_type=MESH,
        ).wait_recv()

    def flip(w, hop, way):
        block = arrived(w, hop, way)
        return pltpu.make_async_remote_copy(
            src_ref=block, dst_ref=block,
            send_sem=flip_send.at[w, hop, way], recv_sem=flip_recv.at[w, hop, way],
            device_id={"ctx": twin}, device_id_type=MESH,
        )

    def flip_wait(w, hop, way):
        source = (pos + chips - hop - 1) % chips if way == 0 else (pos + hop + 1) % chips
        block = full(w).at[chip_of(source, chips) * 2 + 1 - core, way]
        pltpu.make_async_remote_copy(
            src_ref=block, dst_ref=block,
            send_sem=flip_send.at[w, hop, way], recv_sem=flip_recv.at[w, hop, way],
            device_id={"ctx": twin}, device_id_type=MESH,
        ).wait_recv()

    def own_flip(w, who):
        return pltpu.make_async_remote_copy(
            src_ref=w_ref.at[w], dst_ref=full(w).at[who],
            send_sem=own_send.at[w], recv_sem=own_recv.at[w],
            device_id={"ctx": twin}, device_id_type=MESH,
        )

    def begin(w):
        ring(w, 0, 0, True).start()
        ring(w, 0, 1, True).start()
        own_flip(w, me).start()

    def advance(w, hop):
        for way in range(2):
            ring_wait(w, hop - 1, way)
            ring(w, hop, way).start()
            flip(w, hop - 1, way).start()

    def finish(w):
        for way in range(2):
            ring_wait(w, hops - 1, way)
            flip(w, hops - 1, way).start()

    def settle(w):
        local_copy(w).wait()
        own_flip(w, twin).wait_recv()

        @pl.loop(0, hops)
        def _(hop):
            for way in range(2):
                flip_wait(w, hop, way)

    def drain(w):
        own_flip(w, me).wait_send()

        @pl.loop(0, hops)
        def _(hop):
            for way in range(2):
                ring(w, hop, way).wait_send()
                flip(w, hop, way).wait_send()

    def lat_copy(k):
        return pltpu.make_async_remote_copy(
            src_ref=lat_ref, dst_ref=lat_all.at[head],
            send_sem=lat_send.at[k - 1], recv_sem=lat_recv.at[k - 1],
            device_id={"head": (head + k) % heads}, device_id_type=MESH,
        )

    def norm():
        mine.wait()
        for k in range(1, heads):
            came = lat_all.at[(head + heads - k) % heads]
            pltpu.make_async_remote_copy(
                src_ref=lat_ref, dst_ref=came,
                send_sem=lat_send.at[k - 1], recv_sem=lat_recv.at[k - 1],
                device_id={"head": (head + k) % heads}, device_id_type=MESH,
            ).wait_recv()
        step = 16

        @pl.loop(0, tok // step)
        def _(i):
            rows = pl.ds(pl.multiple_of(i * step, step), step)
            squares = jnp.zeros((step, 1), jnp.float32)
            crossed = jnp.zeros((step, 1), jnp.float32)
            for h in range(heads):
                part = lat_all[h, rows, :].astype(jnp.float32)
                tang = probe_ref[rows, h * own:(h + 1) * own].astype(jnp.float32)
                squares = squares + jnp.sum(part * part, -1, keepdims=True)
                crossed = crossed + jnp.sum(part * tang, -1, keepdims=True)
            inverse = lax.rsqrt(squares / D + 1e-06)
            along = crossed / D
            second = inverse * inverse * inverse * along
            rows_t = pl.ds(pl.multiple_of(tok + i * step, step), step)
            for h in range(heads):
                part = lat_all[h, rows, :].astype(jnp.float32)
                tang = probe_ref[rows, h * own:(h + 1) * own].astype(jnp.float32)
                gain = gain_ref[:, h * own:(h + 1) * own]
                x_ref[rows, h * own:(h + 1) * own] = (part * inverse * gain).astype(jnp.bfloat16)
                x_ref[rows_t, h * own:(h + 1) * own] = (
                    (tang * inverse - part * second) * gain
                ).astype(jnp.bfloat16)

    def load(w, piece, slot):
        at = pl.ds(pl.multiple_of(piece * width, width), width)
        return pltpu.make_async_copy(
            qkv_ref.at[w, :, :, :, at], wbuf.at[slot], load_sem.at[slot]
        )

    def multiply(w, piece, slot):
        load(w, piece, slot).wait()
        weight = wbuf[slot].reshape(D, width)
        rows = 128

        @pl.loop(0, 2 * tok // rows)
        def _(i):
            at = pl.ds(pl.multiple_of(i * rows, rows), rows)
            obuf[slot, at, :] = jnp.dot(
                x_ref[at, :], weight, preferred_element_type=jnp.float32
            ).astype(jnp.bfloat16)

        at = pl.ds(pl.multiple_of(piece * width, width), width)
        store = pltpu.make_async_copy(
            obuf.at[slot], proj_ref.at[w, :, at], store_sem.at[slot]
        )
        store.start()
        store.wait()

    def fetch(q, slot):
        @pl.when(q < 2 * pieces)
        def _():
            load(q // pieces, q % pieces, slot).start()

    def work(q, slot):
        @pl.when(q < 2 * pieces)
        def _():
            multiply(q // pieces, q % pieces, slot)

    def halo(side, a):
        return pltpu.make_async_remote_copy(
            src_ref=proj_ref.at[a], dst_ref=halo_ref.at[side, a],
            send_sem=halo_send.at[side, a], recv_sem=halo_recv.at[side, a],
            device_id={"ctx": right if side == 0 else left}, device_id_type=MESH,
        )

    def halo_fill(side, a):
        return pltpu.make_async_copy(proj_ref.at[a], halo_ref.at[side, a], halo_local.at[a])

    def halo_start(a):
        @pl.when(me < n - 1)
        def _():
            halo(0, a).start()

        @pl.when(me > 0)
        def _():
            halo(1, a).start()

        @pl.when(me == 0)
        def _():
            halo_fill(0, a).start()

        @pl.when(me == n - 1)
        def _():
            halo_fill(1, a).start()

    def halo_end(a):
        @pl.when(me < n - 1)
        def _():
            halo(0, a).wait_send()
            halo(1, a).wait_recv()

        @pl.when(me > 0)
        def _():
            halo(1, a).wait_send()
            halo(0, a).wait_recv()

        @pl.when(me == 0)
        def _():
            halo_fill(0, a).wait()

        @pl.when(me == n - 1)
        def _():
            halo_fill(1, a).wait()

    begin(0)
    begin(1)
    for k in range(1, heads):
        lat_copy(k).start()

    @pl.loop(1, hops)
    def _(hop):
        advance(0, hop)
        advance(1, hop)

        @pl.when(hop == hops - 1)
        def _():
            norm()

    begin(2)
    begin(3)
    finish(0)
    finish(1)
    settle(0)
    settle(1)

    @pl.loop(1, hops)
    def _(hop):
        q = (hop - 1) * 4
        fetch(q, 0)
        fetch(q + 1, 1)
        advance(2, hop)
        work(q, 0)
        fetch(q + 2, 0)
        work(q + 1, 1)
        fetch(q + 3, 1)
        advance(3, hop)
        work(q + 2, 0)
        work(q + 3, 1)
        for a in range(2):

            @pl.when(hop == -(-(a + 1) * pieces // 4))
            def _(a=a):
                halo_start(a)

    finish(2)
    finish(3)
    settle(2)

    load(2, 0, 0).start()
    for piece in range(pieces):
        if piece + 1 < pieces:
            load(2, piece + 1, (piece + 1) % 2).start()
        multiply(2, piece, piece % 2)

    settle(3)
    halo_end(0)
    halo_end(1)
    for w in range(4):
        drain(w)
    for k in range(1, heads):
        lat_copy(k).wait_send()


def gather_and_project(latent, probe, gain, weights):
    n = lax.axis_size("ctx")
    heads = lax.axis_size("head")
    hops = n // 2 - 1
    tok, own = latent.shape
    rows, cols = weights.shape[1:]
    weights = weights.reshape(4, 2, rows // 2, cols)
    width = 256 if cols % 256 == 0 else 128
    dma = pltpu.SemaphoreType.DMA
    bf = jnp.bfloat16
    vmem = pl.BlockSpec(memory_space=pltpu.VMEM)
    anywhere = pl.BlockSpec(memory_space=pl.ANY)
    return pl.pallas_call(
        functools.partial(project_kernel, n, heads),
        out_shape=(
            jax.ShapeDtypeStruct((3, n, 2, rows // 2, cols), bf),
            jax.ShapeDtypeStruct((n, 2, rows // 2, cols), bf),
            jax.ShapeDtypeStruct((3, 2 * tok, cols), bf),
            jax.ShapeDtypeStruct((2, 2, 2 * tok, cols), bf),
        ),
        in_specs=[vmem, vmem, vmem, anywhere],
        out_specs=(anywhere,) * 4,
        scratch_shapes=[
            pltpu.VMEM((heads, tok, own), bf),
            pltpu.VMEM((2 * tok, D), bf),
            pltpu.VMEM((2, n, 2, rows // 2, width), bf),
            pltpu.VMEM((2, 2 * tok, width), bf),
            dma((4,)), dma((4, hops, 2)), dma((4, hops, 2)), dma((4, hops, 2)), dma((4, hops, 2)),
            dma((4,)), dma((4,)),
            dma((heads - 1,)), dma((heads - 1,)), dma, dma((2,)), dma((2,)),
            dma((2, 2)), dma((2, 2)), dma((2,)),
        ],
        compiler_params=pltpu.CompilerParams(
            collective_id=0, has_side_effects=True, vmem_limit_bytes=48 * MIB
        ),
    )(latent, probe, gain, weights)


def attend_kernel(tiles, mask_ref, q_ref, own_ref, low_ref, high_ref, out_ref, k_all, v_all):
    tok = tiles * TILE
    scale = HD ** (-0.5)
    for place, ref in enumerate((low_ref, own_ref, high_ref)):
        at = slice(place * tok, (place + 1) * tok)
        k_all[at, :HD] = ref[0, :tok, :]
        k_all[at, HD:] = ref[0, tok:, :]
        v_all[at, :HD] = ref[1, :tok, :]
        v_all[at, HD:] = ref[1, tok:, :]
    contract = (((1,), (1,)), ((), ()))
    band = 2 * tiles + 1
    for i in range(tiles):
        rows = slice(i * TILE, (i + 1) * TILE)
        rows_t = slice(tok + i * TILE, tok + (i + 1) * TILE)
        query = q_ref[0, rows, :]
        query_t = q_ref[0, rows_t, :]
        keys = k_all[i * TILE:(i + band) * TILE, :]
        scores = lax.dot_general(
            query, keys[:, :HD], contract, preferred_element_type=jnp.float32
        ) * scale
        scores_t = lax.dot_general(
            jnp.concatenate([query_t, query], 1), keys, contract,
            preferred_element_type=jnp.float32,
        ) * scale
        masked = jnp.concatenate(
            [
                jnp.where(
                    mask_ref[i, i + j] == 1, scores[:, j * TILE:(j + 1) * TILE], -1e30
                )
                for j in range(band)
            ],
            1,
        )
        highest = jnp.max(masked, -1, keepdims=True)
        expos = jnp.exp(masked - highest)
        probs = expos * (1.0 / jnp.sum(expos, -1, keepdims=True))
        weighed = probs * scores_t
        probs_t = weighed - probs * jnp.sum(weighed, -1, keepdims=True)
        probs_b = probs.astype(jnp.bfloat16)
        values = v_all[i * TILE:(i + band) * TILE, :]
        first = jnp.dot(probs_b, values, preferred_element_type=jnp.float32)
        second = first[:, HD:] + jnp.dot(
            probs_t.astype(jnp.bfloat16), values[:, :HD], preferred_element_type=jnp.float32
        )
        out_ref[rows, :] = first[:, :HD].astype(jnp.bfloat16)
        out_ref[rows_t, :] = second.astype(jnp.bfloat16)


def attend(tile_rows, proj, halo):
    rows, cols = proj.shape[1:]
    tok = rows // 2
    tiles = tok // TILE
    return pl.pallas_call(
        functools.partial(attend_kernel, tiles),
        grid=(cols // HD,),
        out_shape=jax.ShapeDtypeStruct((rows, cols), jnp.bfloat16),
        in_specs=[
            pl.BlockSpec(memory_space=pltpu.SMEM),
            pl.BlockSpec((1, rows, HD), lambda h: (2, 0, h)),
            pl.BlockSpec((2, rows, HD), lambda h: (0, 0, h)),
            pl.BlockSpec((None, 2, rows, HD), lambda h: (0, 0, 0, h)),
            pl.BlockSpec((None, 2, rows, HD), lambda h: (1, 0, 0, h)),
        ],
        out_specs=pl.BlockSpec((rows, HD), lambda h: (0, h)),
        scratch_shapes=[pltpu.VMEM((3 * tok, 2 * HD), jnp.bfloat16)] * 2,
        compiler_params=pltpu.CompilerParams(vmem_limit_bytes=32 * MIB),
    )(tile_rows, proj, proj, halo, halo)


def shards(latent, probe, norm_gain, w_query, w_key, w_value, w_out, tile_mask):
    tok_rows, own_cols = latent.shape
    weights = jnp.stack([w_key, w_value, w_query, w_out.T])
    _, wo_full, proj, halo = gather_and_project(latent, probe, norm_gain.reshape(1, D), weights)
    tiles_dev = tok_rows // TILE
    ctx_slot = lax.axis_index("ctx")
    mask_pad = jnp.pad(tile_mask, tiles_dev)
    tile_rows = lax.dynamic_slice(
        mask_pad,
        (ctx_slot * tiles_dev + tiles_dev, ctx_slot * tiles_dev),
        (tiles_dev, 3 * tiles_dev),
    )
    both_rows = attend(tile_rows, proj, halo)
    w_out_t = wo_full.reshape(D, w_out.shape[0])
    terms = lax.dot_general(
        both_rows, w_out_t, (((1,), (1,)), ((), ())), preferred_element_type=jnp.float32
    ).astype(jnp.bfloat16)
    summed = lax.psum_scatter(terms, "head", scatter_dimension=1, tiled=True).astype(jnp.float32)
    branch = summed[:tok_rows]
    branch_t = summed[tok_rows:]
    latent_f = latent.astype(jnp.float32)
    col_start = lax.axis_index("head") * own_cols
    tangent_own = lax.dynamic_slice_in_dim(probe, col_start, own_cols, 1).astype(jnp.float32)
    mixed = (latent_f + branch).astype(jnp.bfloat16)
    trace_terms = lax.psum(jnp.sum(tangent_own * branch_t, -1), "head")
    return (mixed, branch_t.astype(jnp.bfloat16), trace_terms)


def solution(mesh):
    placed = (
        P("ctx", "head"),
        P("ctx", None),
        P(),
        P("ctx", "head"),
        P("ctx", "head"),
        P("ctx", "head"),
        P("head", "ctx"),
        P(),
    )
    return jax.shard_map(
        shards,
        mesh=mesh,
        in_specs=placed,
        out_specs=(P("ctx", "head"), P("ctx", "head"), P("ctx")),
        check_vma=False,
    )
```
